256 devices in a mesh: row: 16 (over z, y_lo), col: 16 (over x, y_hi, core).
Axes of the slice: x: 4, y: 4 (y_hi: 2, y_lo: 2; y = y_hi * 2 + y_lo), z: 8, core: 2. Of those that a mesh axis runs over, the one named last changes fastest.
Arguments:
- raw: int32 [32768, 4096], P('col', 'row'), may hold values from -128 to 127
- taps: int32 [16, 128], replicated, may hold values from -256 to 256
Outputs:
- visibility: bfloat16 [32, 4096, 2, 4096], P(None, 'row', None, 'col')
The draws below stay inside these ranges and needn't reach their ends.
All inputs are finite; a program needn't handle non-finite values.
Results may differ from the reference program's by a relative error of at most 0.0056.
Values may be sent and summed in bfloat16 or wider, within the bound.
A program may use at most 128 MiB of HBM per device.

```python
import math
import jax
import jax.numpy as jnp
from jax import lax

INPUTS = 4096
CHANNELS = 32
TRANSFORM = 128
TAPS = 16
BLOCKS = 2
SPECTRA = 256
SAMPLES = 32768


def place_ends(array, own_key, low, top_value):
    place = [jax.random.randint(jax.random.fold_in(own_key, axis), (), 0, length) for axis, length in enumerate(array.shape)]
    widest = array.shape.index(max(array.shape))
    beside = place[:widest] + [(place[widest] + 1) % array.shape[widest]] + place[widest + 1:]
    return array.at[tuple(place)].set(low).at[tuple(beside)].set(top_value)


def setup_inputs(seed: int = 0) -> dict:
    keys = jax.random.split(jax.random.key(seed), 3)
    raw = place_ends(jax.random.randint(keys[0], (SAMPLES, INPUTS), -128, 128), jax.random.fold_in(keys[0], 1), -128, 127).astype(jnp.int32)
    taps = place_ends(jax.random.randint(keys[1], (TAPS, TRANSFORM), -256, 257), jax.random.fold_in(keys[1], 1), -256, 256).astype(jnp.int32)
    return dict(raw=raw, taps=taps)


def dft_table():
    sample = jnp.arange(TRANSFORM, dtype=jnp.int32)[:, None]
    channel = jnp.arange(1, CHANNELS + 1, dtype=jnp.int32)[None, :]
    phase = (sample * channel % TRANSFORM).astype(jnp.float32) * (2.0 * math.pi / TRANSFORM)
    return jnp.concatenate([jnp.cos(phase), -jnp.sin(phase)], axis=1)

def channelize(extended, taps, count):
    coeffs = taps.astype(jnp.float32)
    weighted = jnp.zeros((count, TRANSFORM, extended.shape[2]), jnp.float32)
    for offset in range(TAPS):
        start = TAPS - 1 - offset
        weighted = weighted + coeffs[offset][None, :, None] * extended[start:start + count].astype(jnp.float32)
    scale = 1.0 / (8192.0 * math.sqrt(TAPS * TRANSFORM))
    spectra = jnp.einsum('sni,nk->ksi', weighted, dft_table(), precision=lax.Precision.HIGHEST) * scale
    return spectra.reshape(2, CHANNELS, count, extended.shape[2]).astype(jnp.bfloat16)

def correlate_channel(pair):
    left_real, left_imag = pair
    width = SPECTRA // BLOCKS
    total = jnp.zeros((INPUTS, 2 * INPUTS), jnp.float32)
    carry = jnp.zeros((INPUTS, 2 * INPUTS), jnp.float32)
    for block in range(BLOCKS):
        real_part = left_real[block * width:(block + 1) * width]
        imag_part = left_imag[block * width:(block + 1) * width]
        left = jnp.concatenate([real_part, imag_part], axis=0)
        right = jnp.concatenate([jnp.concatenate([real_part, imag_part], axis=0), jnp.concatenate([-imag_part, real_part], axis=0)], axis=1)
        term = lax.dot_general(left, right, (((0,), (0,)), ((), ())), preferred_element_type=jnp.float32)
        if block == 0:
            total = term
        else:
            shifted = term - carry
            summed = total + shifted
            carry = summed - total - shifted
            total = summed
    return (total * (1.0 / SPECTRA)).astype(jnp.bfloat16)

def reference(raw, taps):
    frames = raw.astype(jnp.bfloat16).reshape(SPECTRA, TRANSFORM, INPUTS)
    extended = jnp.concatenate([jnp.zeros((TAPS - 1, TRANSFORM, INPUTS), jnp.bfloat16), frames], axis=0)
    spectra = channelize(extended, taps, SPECTRA)
    result = lax.map(correlate_channel, (spectra[0], spectra[1]))
    return result.reshape(CHANNELS, INPUTS, 2, INPUTS)
```

```python
import math

import jax
import jax.numpy as jnp
from jax import lax
from jax.sharding import PartitionSpec as P

CHANNELS = 32
TRANSFORM = 128
TAPS = 16
SPECTRA_DEV = 16
BLOCKS = 2


def from_behind(block, axis, distance):
    devices = range(lax.axis_size(axis))
    route = [(i - distance, i) for i in devices if i - distance in devices]
    return lax.ppermute(block, axis, route)


def swap_block(block):
    size = lax.axis_size("row")
    route = [(i * size + j, j * size + i) for i in range(size) for j in range(size)]
    return lax.ppermute(block, ("row", "col"), route)


def dft_table():
    sample = jnp.arange(TRANSFORM, dtype=jnp.int32)[:, None]
    channel = jnp.arange(1, CHANNELS + 1, dtype=jnp.int32)[None, :]
    phase = (sample * channel % TRANSFORM).astype(jnp.float32) * (2.0 * math.pi / TRANSFORM)
    return jnp.concatenate([jnp.cos(phase), -jnp.sin(phase)], axis=1)


def channelize(extended, taps, count):
    coeffs = taps.astype(jnp.float32)
    weighted = jnp.zeros((count, TRANSFORM, extended.shape[2]), jnp.float32)
    for offset in range(TAPS):
        start = TAPS - 1 - offset
        weighted = weighted + coeffs[offset][None, :, None] * extended[
            start : start + count
        ].astype(jnp.float32)
    scale = 1.0 / (8192.0 * math.sqrt(TAPS * TRANSFORM))
    spectra = (
        jnp.einsum("sni,nk->ksi", weighted, dft_table(), precision=lax.Precision.HIGHEST) * scale
    )
    return spectra.reshape(2, CHANNELS, count, extended.shape[2]).astype(jnp.bfloat16)


def correlate(row_block, column_block):
    spectra_all = row_block.shape[2]
    width = spectra_all // BLOCKS
    total = None
    for block in range(BLOCKS):
        left = jnp.concatenate(
            [
                row_block[0, :, block * width : (block + 1) * width],
                row_block[1, :, block * width : (block + 1) * width],
            ],
            axis=1,
        )
        real_part = column_block[0, :, block * width : (block + 1) * width]
        imag_part = column_block[1, :, block * width : (block + 1) * width]
        right = jnp.concatenate(
            [
                jnp.concatenate([real_part, imag_part], axis=1),
                jnp.concatenate([-imag_part, real_part], axis=1),
            ],
            axis=2,
        )
        term = lax.dot_general(
            left, right, (((1,), (1,)), ((0,), (0,))), preferred_element_type=jnp.float32
        )
        if block == 0:
            total = term
        else:
            summed = total + term
            total = summed
    result = (total * (1.0 / spectra_all)).astype(jnp.bfloat16)
    return result.reshape(CHANNELS, row_block.shape[3], 2, column_block.shape[3])


def body(raw, taps):
    frames = raw.astype(jnp.bfloat16).reshape(SPECTRA_DEV, TRANSFORM, raw.shape[1])
    rim_frames = frames[SPECTRA_DEV - (TAPS - 1) :]
    earlier = from_behind(rim_frames, "col", 1)
    extended = jnp.concatenate([earlier, frames], axis=0)
    pieces = channelize(extended, taps, SPECTRA_DEV)
    swapped = swap_block(pieces)
    row_block = lax.all_gather(pieces, "col", axis=2, tiled=True)
    column_block = lax.all_gather(swapped, "row", axis=2, tiled=True)
    return correlate(row_block, column_block)


def solution(mesh):
    placed = (P("col", "row"), P())
    return jax.shard_map(
        body, mesh=mesh, in_specs=placed, out_specs=P(None, "row", None, "col"), check_vma=False
    )
```

```python
import math

import jax
import jax.numpy as jnp
import ml_dtypes
import numpy as np
from jax import lax
from jax.experimental import pallas as pl
from jax.experimental.pallas import tpu as pltpu
from jax.sharding import PartitionSpec as P

CHANNELS = 32
TRANSFORM = 128
TAPS = 16
SPECTRA_DEV = 16
SPECTRA = 256
UNITS = 2 * CHANNELS
SIDE = 256
LAG = 8
SPLIT = 2
GROUP = 2
GROUPS = UNITS // GROUP
LEAD = 4
END = 8 * LAG // 2
RIM = TAPS - 1
STRIPS = [(11, 15), (7, 11), (3, 7), (0, 3)]
MESH = pl.DeviceIdType.MESH


def dft_tables():
    sample = np.arange(TRANSFORM)[None, :]
    channel = np.arange(1, CHANNELS + 1)[:, None]
    phase = (sample * channel % TRANSFORM) * (2.0 * math.pi / TRANSFORM)
    rest = np.stack([np.cos(phase), -np.sin(phase)], axis=1).reshape(UNITS, TRANSFORM)
    rest = rest.astype(np.float32)
    parts = []
    for _ in range(3):
        part = rest.astype(ml_dtypes.bfloat16)
        rest = rest - part.astype(np.float32)
        parts.append(part)
    one, two, three = parts
    first = np.block([[one, one], [three, two]])
    second = np.block([[two, one]])
    return np.concatenate([first, second], axis=0)


def product(a, b):
    return lax.dot_general(a, b, (((0,), (0,)), ((), ())), preferred_element_type=jnp.float32)


def own_filter(raw_ref, taps_ref, acc):
    def tile(i, carry):
        rows = pl.multiple_of(i * 8, 8)
        for half in range(2):
            lanes = pl.ds(half * 128, 128)
            taps = [taps_ref[p, pl.ds(rows, 8), :] for p in range(TAPS)]
            frames = [
                raw_ref[pl.ds(s * TRANSFORM + rows, 8), lanes].astype(jnp.float32)
                for s in range(SPECTRA_DEV)
            ]
            for s in range(SPECTRA_DEV):
                total = taps[0] * frames[s]
                for p in range(1, s + 1):
                    total = total + taps[p] * frames[s - p]
                acc[s, pl.ds(rows, 8), lanes] = total
        return carry

    lax.fori_loop(0, TRANSFORM // 8, tile, 0)


def rim_filter(low, high, rim, taps_ref, acc):
    def tile(i, carry):
        rows = pl.multiple_of(i * 16, 16)
        for half in range(2):
            lanes = pl.ds(half * 128, 128)
            frames = [
                rim[j, pl.ds(rows, 16), lanes].astype(jnp.float32) for j in range(low, high)
            ]
            for s in range(high):
                total = acc[s, pl.ds(rows, 16), lanes]
                for j in range(max(s, low), high):
                    tap = taps_ref[RIM + s - j, pl.ds(rows, 16), :]
                    total = total + tap * frames[j - low]
                acc[s, pl.ds(rows, 16), lanes] = total
        return carry

    lax.fori_loop(0, TRANSFORM // 16, tile, 0)


def spread_taps(table_ref, spread):
    taps = table_ref[3 * UNITS :, :TRANSFORM]
    index = lax.broadcasted_iota(jnp.int32, (TAPS, 128), 0)
    for p in range(TAPS):
        pick = jnp.where(index == p, 1.0, 0.0).astype(jnp.bfloat16)
        spread[p] = product(taps, pick)


def transform(low, high, table_ref, acc, flat):
    scale = 1.0 / (8192.0 * math.sqrt(TAPS * TRANSFORM))

    def one(s, carry):
        value = acc[s]
        high = value.astype(jnp.bfloat16)
        rest = value - high.astype(jnp.float32)
        mid = rest.astype(jnp.bfloat16)
        low = (rest - mid.astype(jnp.float32)).astype(jnp.bfloat16)
        most = jnp.dot(
            table_ref[: 2 * UNITS, :], jnp.concatenate([high, mid], axis=0),
            preferred_element_type=jnp.float32,
        )
        less = jnp.dot(
            table_ref[2 * UNITS : 3 * UNITS, :], jnp.concatenate([high, low], axis=0),
            preferred_element_type=jnp.float32,
        )
        result = (most[:UNITS] + (less + most[UNITS:])) * scale
        rows = pl.ds(pl.multiple_of(s * UNITS, UNITS), UNITS)
        for half in range(2):
            flat[half, rows, :] = result[:, half * 128 : (half + 1) * 128]
        return carry

    lax.fori_loop(low, high, one, 0)


def gather_correlate(
    raw_ref, table_ref, o_ref, a, b, rim, own_rim, acc, flat, taps_ref, rim_sem, y_sem, x_sem,
    s_sem, z_sem, f_sem, out_sem,
):
    r = lax.axis_index("row")
    c = lax.axis_index("col")
    z, yl = r // 2, r % 2
    x, yh, co = c // 4, (c // 2) % 2, c % 2
    flip_r = r + 1 - 2 * yl
    at_x = 2 * x
    place = at_x + yh
    rest = pl.ds(0, SPLIT)
    far = pl.ds(SPLIT, 8 - SPLIT)
    flip_y = c + 2 - 4 * yh
    flip_core = c + 1 - 2 * co
    z_next = [((r + 2) % 16, c), ((r + 14) % 16, c)]
    x_next = [(r, (c + 4 * d) % 16) for d in (1, 2, 3)]
    pair = (flip_r, c)
    cross = (flip_r, flip_y)
    sibling = (r, flip_core)
    across = (r, flip_y)

    barrier = pltpu.get_barrier_semaphore()
    after = (r, (c + 1) % 16)
    before = (r, (c + 15) % 16)
    for peer in z_next + x_next + [pair, cross, sibling, across, after, before]:
        pl.semaphore_signal(barrier, inc=1, device_id=peer, device_id_type=MESH)
    spread_taps(table_ref, taps_ref)
    for s in range(RIM):
        own_rim[s] = raw_ref[(s + 1) * TRANSFORM : (s + 2) * TRANSFORM, :].astype(jnp.bfloat16)
    pl.semaphore_wait(barrier, 11)

    dz = (z - c // 2 + 8) % 8
    main = yl == co
    root = jnp.logical_and(main, dz == 0)
    helper = r == flip_y
    hops = dz + jnp.where(main, 0, 1)
    back = (8 - dz) % 8 + jnp.where(main, 0, 1)
    begin = [LAG * hops // 2, LAG * back // 2]
    more = [dz != 7, dz != 1]

    def remote(src, dst, send, recv, peer):
        return pltpu.make_async_remote_copy(
            src_ref=src, dst_ref=dst, send_sem=send, recv_sem=recv, device_id=peer,
            device_id_type=MESH,
        )

    def arrived(dst, sem):
        remote(dst, dst, sem, sem, pair).wait_recv()

    def strip_copy(q):
        frames = pl.ds(STRIPS[q][0], STRIPS[q][1] - STRIPS[q][0])
        return remote(
            own_rim.at[frames], rim.at[frames], out_sem.at[11], rim_sem.at[q], after
        )

    @pl.when(c < 15)
    def _():
        for q in range(len(STRIPS)):
            strip_copy(q).start()

    @pl.when(c == 0)
    def _():
        rim[...] = jnp.zeros_like(rim)

    own_filter(raw_ref, taps_ref, acc)
    done = SPECTRA_DEV
    for q, (low, high) in enumerate(STRIPS):
        @pl.when(c > 0)
        def _():
            strip_copy(q).wait_recv()

        rim_filter(low, high, rim, taps_ref, acc)
        transform(low, done, table_ref, acc, flat)
        done = low

    def send_across(j, carry):
        for e in range(GROUP):
            u = j * GROUP + e
            for half in range(2):
                lanes = pl.ds(half * 128, 128)
                rows = flat[half, pl.ds(u, SPECTRA_DEV, stride=UNITS), :]
                a[u, co, place, :, lanes] = rows.astype(jnp.bfloat16)
        rows = pl.ds(j * GROUP, GROUP)
        remote(
            a.at[rows, co, place], a.at[rows, co, place], out_sem.at[0], y_sem.at[j], across
        ).start()
        return carry

    lax.fori_loop(0, GROUPS, send_across, 0)

    def step(i, carry):
        t = i - 2 * LEAD

        @pl.when(jnp.logical_and(t % GROUP == 0, t < UNITS))
        def _():
            j = t // GROUP

            @pl.when(t >= 0)
            def _():
                arrived(a.at[pl.ds(j * GROUP, GROUP), 1 - co], s_sem.at[j])

            m = j + 2 * LEAD // GROUP

            @pl.when(m < GROUPS)
            def _():
                rows = pl.ds(m * GROUP, GROUP)
                arrived(a.at[rows, co, at_x + 1 - yh], y_sem.at[m])
                for d in range(3):
                    remote(
                        a.at[rows, co, pl.ds(at_x, 2)], a.at[rows, co, pl.ds(at_x, 2)], out_sem.at[1 + d],
                        x_sem.at[d, m], x_next[d],
                    ).start()

            n = j + LEAD // GROUP

            @pl.when(jnp.logical_and(n >= 0, n < GROUPS))
            def _():
                rows = pl.ds(n * GROUP, GROUP)
                for d in range(3):
                    arrived(a.at[rows, co, pl.ds((x + 3 - d) % 4 * 2, 2)], x_sem.at[d, n])
                remote(
                    a.at[rows, co], a.at[rows, co], out_sem.at[4], s_sem.at[n], sibling
                ).start()

        for h in range(2):
            u = t - begin[h]

            @pl.when(jnp.logical_and(u >= 0, u < UNITS))
            def _():
                @pl.when(root)
                def _():
                    remote(
                        a.at[u, h], b.at[u, h], out_sem.at[5 + h], z_sem.at[h, u], z_next[h]
                    ).start()
                    remote(
                        a.at[u, h, rest], b.at[u, h, rest], out_sem.at[7 + h], z_sem.at[h, u], pair
                    ).start()
                    pltpu.make_async_copy(a.at[u, h], b.at[u, h], f_sem.at[h, u]).start()

                @pl.when(jnp.logical_and(main, jnp.logical_not(root)))
                def _():
                    arrived(b.at[u, h], z_sem.at[h, u])

                    @pl.when(more[h])
                    def _():
                        remote(
                            b.at[u, h], b.at[u, h], out_sem.at[5 + h], z_sem.at[h, u], z_next[h]
                        ).start()

                    remote(
                        b.at[u, h, far], b.at[u, h, far], out_sem.at[7 + h], f_sem.at[h, u], pair
                    ).start()

                @pl.when(jnp.logical_not(main))
                def _():
                    arrived(b.at[u, h, rest], z_sem.at[h, u])

                    @pl.when(more[h])
                    def _():
                        remote(
                            b.at[u, h, rest], b.at[u, h, rest], out_sem.at[5 + h], z_sem.at[h, u],
                            z_next[h],
                        ).start()

        @pl.when(jnp.logical_and(helper, jnp.logical_and(t >= 0, t < UNITS)))
        def _():
            for h in range(2):
                remote(
                    a.at[t, h, far], b.at[t, h, far], out_sem.at[9 + h], f_sem.at[h, t], cross
                ).start()

        v = t - END - 1

        @pl.when(jnp.logical_and(v >= 0, v % 2 == 0))
        def _():
            for e in range(2):
                for h in range(2):
                    @pl.when(root)
                    def _():
                        pltpu.make_async_copy(
                            a.at[v + e, h], b.at[v + e, h], f_sem.at[h, v + e]
                        ).wait()

                    @pl.when(jnp.logical_not(main))
                    def _():
                        arrived(b.at[v + e, h, far], f_sem.at[h, v + e])

            a_re = a[v].reshape(SIDE, SIDE)
            a_im = a[v + 1].reshape(SIDE, SIDE)
            b_re = b[v].reshape(SIDE, SIDE)
            b_im = b[v + 1].reshape(SIDE, SIDE)
            real = product(a_re, b_re) + product(a_im, b_im)
            imag = product(a_im, b_re) - product(a_re, b_im)
            k = v // 2
            o_ref[k, :, 0, :] = (real * (1.0 / SPECTRA)).astype(jnp.bfloat16)
            o_ref[k, :, 1, :] = (imag * (1.0 / SPECTRA)).astype(jnp.bfloat16)

        return carry

    lax.fori_loop(0, UNITS + END + 2 * LEAD, step, 0)

    def left(src, sem):
        remote(src, src, sem, sem, pair).wait_send()

    @pl.when(c < 15)
    def _():
        left(own_rim, out_sem.at[11])

    left(a.at[:, co, place], out_sem.at[0])
    for d in range(3):
        left(a.at[:, co, pl.ds(at_x, 2)], out_sem.at[1 + d])
    left(a.at[:, co], out_sem.at[4])
    for h in range(2):
        @pl.when(jnp.logical_and(main, more[h]))
        def _():
            left(b.at[:, h], out_sem.at[5 + h])

        @pl.when(jnp.logical_and(jnp.logical_not(main), more[h]))
        def _():
            left(b.at[:, h, rest], out_sem.at[5 + h])

        @pl.when(root)
        def _():
            left(b.at[:, h, rest], out_sem.at[7 + h])

        @pl.when(jnp.logical_and(main, jnp.logical_not(root)))
        def _():
            left(b.at[:, h, far], out_sem.at[7 + h])

        @pl.when(helper)
        def _():
            left(a.at[:, h, far], out_sem.at[9 + h])


def body(raw, taps):
    wide = jnp.concatenate([taps, jnp.zeros_like(taps)], axis=1).astype(jnp.bfloat16)
    table = jnp.concatenate([dft_tables(), wide], axis=0)
    block = (UNITS, 2, 8, SPECTRA_DEV, SIDE)
    dma = pltpu.SemaphoreType.DMA
    return pl.pallas_call(
        gather_correlate,
        out_shape=jax.ShapeDtypeStruct((CHANNELS, SIDE, 2, SIDE), jnp.bfloat16),
        in_specs=[pl.BlockSpec(memory_space=pltpu.VMEM)] * 2,
        out_specs=pl.BlockSpec(memory_space=pltpu.VMEM),
        scratch_shapes=[
            pltpu.VMEM(block, jnp.bfloat16),
            pltpu.VMEM(block, jnp.bfloat16),
            pltpu.VMEM((RIM, TRANSFORM, SIDE), jnp.bfloat16),
            pltpu.VMEM((RIM, TRANSFORM, SIDE), jnp.bfloat16),
            pltpu.VMEM((SPECTRA_DEV, TRANSFORM, SIDE), jnp.float32),
            pltpu.VMEM((2, SPECTRA_DEV * UNITS, 128), jnp.float32),
            pltpu.VMEM((TAPS, TRANSFORM, 128), jnp.float32),
            dma((len(STRIPS),)),
            dma((GROUPS,)),
            dma((3, GROUPS)),
            dma((GROUPS,)),
            dma((2, UNITS)),
            dma((2, UNITS)),
            dma((12,)),
        ],
        compiler_params=pltpu.CompilerParams(
            collective_id=0, has_side_effects=True, vmem_limit_bytes=30 * 1024 * 1024
        ),
    )(raw, table)


def solution(mesh):
    placed = (P("col", "row"), P())
    return jax.shard_map(
        body, mesh=mesh, in_specs=placed, out_specs=P(None, "row", None, "col"), check_vma=False
    )
```

```python
import math

import jax
import jax.numpy as jnp
import ml_dtypes
import numpy as np
from jax import lax
from jax.experimental import pallas as pl
from jax.experimental.pallas import tpu as pltpu
from jax.sharding import PartitionSpec as P

CHANNELS = 32
TRANSFORM = 128
TAPS = 16
SPECTRA_DEV = 16
SPECTRA = 256
UNITS = 2 * CHANNELS
SIDE = 256
LAG = 8
SPLIT = 2
GROUP = 2
GROUPS = UNITS // GROUP
LEAD = 6
END = 8 * LAG // 2
TAIL = UNITS - 6
TAIL_END = 5 * LAG // 2 + 4
RIM = TAPS - 1
STRIPS = [(11, 15), (7, 11), (3, 7), (0, 3)]
MESH = pl.DeviceIdType.MESH


def dft_tables():
    sample = np.arange(TRANSFORM)[None, :]
    channel = np.arange(1, CHANNELS + 1)[:, None]
    phase = (sample * channel % TRANSFORM) * (2.0 * math.pi / TRANSFORM)
    rest = np.stack([np.cos(phase), -np.sin(phase)], axis=1).reshape(UNITS, TRANSFORM)
    rest = rest.astype(np.float32)
    parts = []
    for _ in range(3):
        part = rest.astype(ml_dtypes.bfloat16)
        rest = rest - part.astype(np.float32)
        parts.append(part)
    one, two, three = parts
    first = np.block([[one, one], [three, two]])
    second = np.block([[two, one]])
    return np.concatenate([first, second], axis=0)


def product(a, b):
    return lax.dot_general(a, b, (((0,), (0,)), ((), ())), preferred_element_type=jnp.float32)


def own_filter(raw_ref, taps_ref, acc):
    def tile(i, carry):
        rows = pl.multiple_of(i * 8, 8)
        for half in range(2):
            lanes = pl.ds(half * 128, 128)
            taps = [taps_ref[p, pl.ds(rows, 8), :] for p in range(TAPS)]
            frames = [
                raw_ref[pl.ds(s * TRANSFORM + rows, 8), lanes].astype(jnp.float32)
                for s in range(SPECTRA_DEV)
            ]
            for s in range(SPECTRA_DEV):
                total = taps[0] * frames[s]
                for p in range(1, s + 1):
                    total = total + taps[p] * frames[s - p]
                acc[s, pl.ds(rows, 8), lanes] = total
        return carry

    lax.fori_loop(0, TRANSFORM // 8, tile, 0)


def rim_filter(low, high, rim, taps_ref, acc):
    def tile(i, carry):
        rows = pl.multiple_of(i * 16, 16)
        for half in range(2):
            lanes = pl.ds(half * 128, 128)
            frames = [
                rim[j, pl.ds(rows, 16), lanes].astype(jnp.float32) for j in range(low, high)
            ]
            for s in range(high):
                total = acc[s, pl.ds(rows, 16), lanes]
                for j in range(max(s, low), high):
                    tap = taps_ref[RIM + s - j, pl.ds(rows, 16), :]
                    total = total + tap * frames[j - low]
                acc[s, pl.ds(rows, 16), lanes] = total
        return carry

    lax.fori_loop(0, TRANSFORM // 16, tile, 0)


def spread_taps(table_ref, spread):
    taps = table_ref[3 * UNITS :, :TRANSFORM]
    index = lax.broadcasted_iota(jnp.int32, (TAPS, 128), 0)
    for p in range(TAPS):
        pick = jnp.where(index == p, 1.0, 0.0).astype(jnp.bfloat16)
        spread[p] = product(taps, pick)


def transform(low, high, table_ref, acc, flat):
    scale = 1.0 / (8192.0 * math.sqrt(TAPS * TRANSFORM))

    def one(s, carry):
        value = acc[s]
        high = value.astype(jnp.bfloat16)
        rest = value - high.astype(jnp.float32)
        mid = rest.astype(jnp.bfloat16)
        low = (rest - mid.astype(jnp.float32)).astype(jnp.bfloat16)
        most = jnp.dot(
            table_ref[: 2 * UNITS, :], jnp.concatenate([high, mid], axis=0),
            preferred_element_type=jnp.float32,
        )
        less = jnp.dot(
            table_ref[2 * UNITS : 3 * UNITS, :], jnp.concatenate([high, low], axis=0),
            preferred_element_type=jnp.float32,
        )
        result = (most[:UNITS] + (less + most[UNITS:])) * scale
        rows = pl.ds(pl.multiple_of(s * UNITS, UNITS), UNITS)
        for half in range(2):
            flat[half, rows, :] = result[:, half * 128 : (half + 1) * 128]
        return carry

    lax.fori_loop(low, high, one, 0)


def gather_correlate(
    raw_ref, table_ref, o_ref, a, b, rim, own_rim, acc, flat, taps_ref, rim_sem, y_sem, x_sem,
    s_sem, z_sem, f_sem, out_sem,
):
    r = lax.axis_index("row")
    c = lax.axis_index("col")
    z, yl = r // 2, r % 2
    x, yh, co = c // 4, (c // 2) % 2, c % 2
    flip_r = r + 1 - 2 * yl
    at_x = 2 * x
    place = at_x + yh
    rest = pl.ds(0, SPLIT)
    far = pl.ds(SPLIT, 8 - SPLIT)
    flip_y = c + 2 - 4 * yh
    flip_core = c + 1 - 2 * co
    z_next = [((r + 2) % 16, c), ((r + 14) % 16, c)]
    x_next = [(r, (c + 4 * d) % 16) for d in (1, 2, 3)]
    pair = (flip_r, c)
    cross = (flip_r, flip_y)
    sibling = (r, flip_core)
    across = (r, flip_y)

    barrier = pltpu.get_barrier_semaphore()
    after = (r, (c + 1) % 16)
    before = (r, (c + 15) % 16)
    for peer in z_next + x_next + [pair, cross, sibling, across, after, before]:
        pl.semaphore_signal(barrier, inc=1, device_id=peer, device_id_type=MESH)
    spread_taps(table_ref, taps_ref)
    for s in range(RIM):
        own_rim[s] = raw_ref[(s + 1) * TRANSFORM : (s + 2) * TRANSFORM, :].astype(jnp.bfloat16)
    pl.semaphore_wait(barrier, 11)

    dz = (z - c // 2 + 8) % 8
    main = yl == co
    root = jnp.logical_and(main, dz == 0)
    helper = r == flip_y
    hops = dz + jnp.where(main, 0, 1)
    back = (8 - dz) % 8 + jnp.where(main, 0, 1)
    begin = [LAG * hops // 2, LAG * back // 2]
    more = [dz != 7, dz != 1]
    source = dz == 0
    tail_hops = jnp.minimum(dz, (8 - dz) % 8) + jnp.where(main, 0, 1)
    tail_begin = LAG * tail_hops // 2
    tail_more = [
        jnp.logical_or(source, jnp.logical_and(dz >= 1, dz <= 3)),
        jnp.logical_or(source, dz >= 6),
    ]

    def remote(src, dst, send, recv, peer):
        return pltpu.make_async_remote_copy(
            src_ref=src, dst_ref=dst, send_sem=send, recv_sem=recv, device_id=peer,
            device_id_type=MESH,
        )

    def arrived(dst, sem):
        remote(dst, dst, sem, sem, pair).wait_recv()

    def strip_copy(q):
        frames = pl.ds(STRIPS[q][0], STRIPS[q][1] - STRIPS[q][0])
        return remote(
            own_rim.at[frames], rim.at[frames], out_sem.at[11], rim_sem.at[q], after
        )

    @pl.when(c < 15)
    def _():
        for q in range(len(STRIPS)):
            strip_copy(q).start()

    @pl.when(c == 0)
    def _():
        rim[...] = jnp.zeros_like(rim)

    own_filter(raw_ref, taps_ref, acc)
    done = SPECTRA_DEV
    for q, (low, high) in enumerate(STRIPS):
        @pl.when(c > 0)
        def _():
            strip_copy(q).wait_recv()

        rim_filter(low, high, rim, taps_ref, acc)
        transform(low, done, table_ref, acc, flat)
        done = low

    def send_across(j, carry):
        for e in range(GROUP):
            u = j * GROUP + e
            for half in range(2):
                lanes = pl.ds(half * 128, 128)
                rows = flat[half, pl.ds(u, SPECTRA_DEV, stride=UNITS), :]
                a[u, co, place, :, lanes] = rows.astype(jnp.bfloat16)
        rows = pl.ds(j * GROUP, GROUP)
        remote(
            a.at[rows, co, place], a.at[rows, co, place], out_sem.at[0], y_sem.at[j], across
        ).start()
        return carry

    lax.fori_loop(0, GROUPS, send_across, 0)

    def step(i, carry):
        t = i - 2 * LEAD

        @pl.when(jnp.logical_and(t % GROUP == 0, t < UNITS))
        def _():
            j = t // GROUP

            @pl.when(t >= 0)
            def _():
                arrived(a.at[pl.ds(j * GROUP, GROUP), 1 - co], s_sem.at[j])

            m = j + 2 * LEAD // GROUP

            @pl.when(m < GROUPS)
            def _():
                rows = pl.ds(m * GROUP, GROUP)
                arrived(a.at[rows, co, at_x + 1 - yh], y_sem.at[m])
                for d in range(3):
                    remote(
                        a.at[rows, co, pl.ds(at_x, 2)], a.at[rows, co, pl.ds(at_x, 2)], out_sem.at[1 + d],
                        x_sem.at[d, m], x_next[d],
                    ).start()

            n = j + LEAD // GROUP

            @pl.when(jnp.logical_and(n >= 0, n < GROUPS))
            def _():
                rows = pl.ds(n * GROUP, GROUP)
                for d in range(3):
                    arrived(a.at[rows, co, pl.ds((x + 3 - d) % 4 * 2, 2)], x_sem.at[d, n])
                remote(
                    a.at[rows, co], a.at[rows, co], out_sem.at[4], s_sem.at[n], sibling
                ).start()

        for h in range(2):
            u = t - begin[h]

            @pl.when(jnp.logical_and(u >= 0, u < TAIL))
            def _():
                @pl.when(root)
                def _():
                    remote(
                        a.at[u, h], b.at[u, h], out_sem.at[5 + h], z_sem.at[h, u], z_next[h]
                    ).start()
                    remote(
                        a.at[u, h, rest], b.at[u, h, rest], out_sem.at[7 + h], z_sem.at[h, u], pair
                    ).start()
                    pltpu.make_async_copy(a.at[u, h], b.at[u, h], f_sem.at[h, u]).start()

                @pl.when(jnp.logical_and(main, jnp.logical_not(root)))
                def _():
                    arrived(b.at[u, h], z_sem.at[h, u])

                    @pl.when(more[h])
                    def _():
                        remote(
                            b.at[u, h], b.at[u, h], out_sem.at[5 + h], z_sem.at[h, u], z_next[h]
                        ).start()

                    remote(
                        b.at[u, h, far], b.at[u, h, far], out_sem.at[7 + h], f_sem.at[h, u], pair
                    ).start()

                @pl.when(jnp.logical_not(main))
                def _():
                    arrived(b.at[u, h, rest], z_sem.at[h, u])

                    @pl.when(more[h])
                    def _():
                        remote(
                            b.at[u, h, rest], b.at[u, h, rest], out_sem.at[5 + h], z_sem.at[h, u],
                            z_next[h],
                        ).start()

        w = t - tail_begin

        @pl.when(jnp.logical_and(w >= TAIL, w < UNITS))
        def _():
            for h in range(2):
                @pl.when(root)
                def _():
                    for d in range(2):
                        remote(
                            a.at[w, h], b.at[w, h], out_sem.at[12 + d], z_sem.at[h, w], z_next[d]
                        ).start()
                    remote(
                        a.at[w, h, rest], b.at[w, h, rest], out_sem.at[7 + h], z_sem.at[h, w], pair
                    ).start()
                    pltpu.make_async_copy(a.at[w, h], b.at[w, h], f_sem.at[h, w]).start()

                @pl.when(jnp.logical_and(main, jnp.logical_not(root)))
                def _():
                    arrived(b.at[w, h], z_sem.at[h, w])
                    for d in range(2):
                        @pl.when(tail_more[d])
                        def _():
                            remote(
                                b.at[w, h], b.at[w, h], out_sem.at[12 + d], z_sem.at[h, w],
                                z_next[d],
                            ).start()

                    remote(
                        b.at[w, h, far], b.at[w, h, far], out_sem.at[7 + h], f_sem.at[h, w], pair
                    ).start()

                @pl.when(jnp.logical_not(main))
                def _():
                    arrived(b.at[w, h, rest], z_sem.at[h, w])
                    for d in range(2):
                        @pl.when(tail_more[d])
                        def _():
                            remote(
                                b.at[w, h, rest], b.at[w, h, rest], out_sem.at[12 + d],
                                z_sem.at[h, w], z_next[d],
                            ).start()

        @pl.when(jnp.logical_and(helper, jnp.logical_and(t >= 0, t < UNITS)))
        def _():
            for h in range(2):
                remote(
                    a.at[t, h, far], b.at[t, h, far], out_sem.at[9 + h], f_sem.at[h, t], cross
                ).start()

        first = t - END - 1
        last = t - TAIL_END
        ends = last % 2 == 0
        v = jnp.where(ends, last, first)

        @pl.when(
            jnp.logical_or(
                jnp.logical_and(ends, jnp.logical_and(last >= TAIL, last < UNITS)),
                jnp.logical_and(jnp.logical_not(ends), jnp.logical_and(first >= 0, first < TAIL)),
            )
        )
        def _():
            for e in range(2):
                for h in range(2):
                    @pl.when(root)
                    def _():
                        pltpu.make_async_copy(
                            a.at[v + e, h], b.at[v + e, h], f_sem.at[h, v + e]
                        ).wait()

                    @pl.when(jnp.logical_not(main))
                    def _():
                        arrived(b.at[v + e, h, far], f_sem.at[h, v + e])

            a_re = a[v].reshape(SIDE, SIDE)
            a_im = a[v + 1].reshape(SIDE, SIDE)
            b_re = b[v].reshape(SIDE, SIDE)
            b_im = b[v + 1].reshape(SIDE, SIDE)
            real = product(a_re, b_re) + product(a_im, b_im)
            imag = product(a_im, b_re) - product(a_re, b_im)
            k = v // 2
            o_ref[k, :, 0, :] = (real * (1.0 / SPECTRA)).astype(jnp.bfloat16)
            o_ref[k, :, 1, :] = (imag * (1.0 / SPECTRA)).astype(jnp.bfloat16)

        return carry

    lax.fori_loop(0, max(TAIL + END, UNITS + TAIL_END) + 2 * LEAD, step, 0)

    def left(src, sem):
        remote(src, src, sem, sem, pair).wait_send()

    @pl.when(c < 15)
    def _():
        left(own_rim, out_sem.at[11])

    left(a.at[:, co, place], out_sem.at[0])
    for d in range(3):
        left(a.at[:, co, pl.ds(at_x, 2)], out_sem.at[1 + d])
    left(a.at[:, co], out_sem.at[4])
    for h in range(2):
        @pl.when(jnp.logical_and(main, more[h]))
        def _():
            left(b.at[pl.ds(0, TAIL), h], out_sem.at[5 + h])

        @pl.when(jnp.logical_and(main, tail_more[h]))
        def _():
            left(b.at[pl.ds(TAIL, UNITS - TAIL)], out_sem.at[12 + h])

        @pl.when(jnp.logical_and(jnp.logical_not(main), tail_more[h]))
        def _():
            left(b.at[pl.ds(TAIL, UNITS - TAIL), :, rest], out_sem.at[12 + h])

        @pl.when(jnp.logical_and(jnp.logical_not(main), more[h]))
        def _():
            left(b.at[pl.ds(0, TAIL), h, rest], out_sem.at[5 + h])

        @pl.when(root)
        def _():
            left(b.at[:, h, rest], out_sem.at[7 + h])

        @pl.when(jnp.logical_and(main, jnp.logical_not(root)))
        def _():
            left(b.at[:, h, far], out_sem.at[7 + h])

        @pl.when(helper)
        def _():
            left(a.at[:, h, far], out_sem.at[9 + h])


def body(raw, taps):
    wide = jnp.concatenate([taps, jnp.zeros_like(taps)], axis=1).astype(jnp.bfloat16)
    table = jnp.concatenate([dft_tables(), wide], axis=0)
    block = (UNITS, 2, 8, SPECTRA_DEV, SIDE)
    dma = pltpu.SemaphoreType.DMA
    return pl.pallas_call(
        gather_correlate,
        out_shape=jax.ShapeDtypeStruct((CHANNELS, SIDE, 2, SIDE), jnp.bfloat16),
        in_specs=[pl.BlockSpec(memory_space=pltpu.VMEM)] * 2,
        out_specs=pl.BlockSpec(memory_space=pltpu.VMEM),
        scratch_shapes=[
            pltpu.VMEM(block, jnp.bfloat16),
            pltpu.VMEM(block, jnp.bfloat16),
            pltpu.VMEM((RIM, TRANSFORM, SIDE), jnp.bfloat16),
            pltpu.VMEM((RIM, TRANSFORM, SIDE), jnp.bfloat16),
            pltpu.VMEM((SPECTRA_DEV, TRANSFORM, SIDE), jnp.float32),
            pltpu.VMEM((2, SPECTRA_DEV * UNITS, 128), jnp.float32),
            pltpu.VMEM((TAPS, TRANSFORM, 128), jnp.float32),
            dma((len(STRIPS),)),
            dma((GROUPS,)),
            dma((3, GROUPS)),
            dma((GROUPS,)),
            dma((2, UNITS)),
            dma((2, UNITS)),
            dma((14,)),
        ],
        compiler_params=pltpu.CompilerParams(
            collective_id=0, has_side_effects=True, vmem_limit_bytes=30 * 1024 * 1024
        ),
    )(raw, table)


def solution(mesh):
    placed = (P("col", "row"), P())
    return jax.shard_map(
        body, mesh=mesh, in_specs=placed, out_specs=P(None, "row", None, "col"), check_vma=False
    )
```

```python
import math

import jax
import jax.numpy as jnp
from jax import lax
from jax.experimental import pallas as pl
from jax.experimental.pallas import tpu as pltpu
from jax.sharding import PartitionSpec as P

CHANNELS = 32
TRANSFORM = 128
TAPS = 16
SPECTRA_DEV = 16
SPECTRA = 256
UNITS = 2 * CHANNELS
SIDE = 256
LAG = 8
SPLIT = 2
GROUP = 2
GROUPS = UNITS // GROUP
LEAD = 6
END = 8 * LAG // 2
TAIL = UNITS - 6
TAIL_END = 5 * LAG // 2 + 4
RIM = TAPS - 1
STRIPS = [(11, 15), (7, 11), (3, 7), (0, 3)]
MESH = pl.DeviceIdType.MESH


def dft_table(table_ref):
    row = lax.broadcasted_iota(jnp.int32, (UNITS, TRANSFORM), 0)
    sample = lax.broadcasted_iota(jnp.int32, (UNITS, TRANSFORM), 1)
    turn = (sample * ((row >> 1) + 1) + (TRANSFORM // 4) * (row & 1)) & (TRANSFORM - 1)
    turn = jnp.minimum(turn, TRANSFORM - turn)
    rest = jnp.cos(turn.astype(jnp.float32) * (2.0 * math.pi / TRANSFORM))
    parts = []
    for _ in range(3):
        part = rest.astype(jnp.bfloat16)
        rest = rest - part.astype(jnp.float32)
        parts.append(part)
    one, two, three = parts
    for i, pair in enumerate(((one, one), (three, two), (two, one))):
        for half in range(2):
            table_ref[i * UNITS : (i + 1) * UNITS, half * TRANSFORM : (half + 1) * TRANSFORM] = (
                pair[half]
            )


def product(a, b):
    return lax.dot_general(a, b, (((0,), (0,)), ((), ())), preferred_element_type=jnp.float32)


def own_filter(raw_ref, taps_ref, acc):
    def tile(i, carry):
        rows = pl.multiple_of(i * 8, 8)
        for half in range(2):
            lanes = pl.ds(half * 128, 128)
            taps = [taps_ref[p, pl.ds(rows, 8), :] for p in range(TAPS)]
            frames = [
                raw_ref[pl.ds(s * TRANSFORM + rows, 8), lanes].astype(jnp.float32)
                for s in range(SPECTRA_DEV)
            ]
            for s in range(SPECTRA_DEV):
                total = taps[0] * frames[s]
                for p in range(1, s + 1):
                    total = total + taps[p] * frames[s - p]
                acc[s, pl.ds(rows, 8), lanes] = total
        return carry

    lax.fori_loop(0, TRANSFORM // 8, tile, 0)


def rim_filter(low, high, rim, taps_ref, acc):
    def tile(i, carry):
        rows = pl.multiple_of(i * 16, 16)
        for half in range(2):
            lanes = pl.ds(half * 128, 128)
            frames = [
                rim[j, pl.ds(rows, 16), lanes].astype(jnp.float32) for j in range(low, high)
            ]
            for s in range(high):
                total = acc[s, pl.ds(rows, 16), lanes]
                for j in range(max(s, low), high):
                    tap = taps_ref[RIM + s - j, pl.ds(rows, 16), :]
                    total = total + tap * frames[j - low]
                acc[s, pl.ds(rows, 16), lanes] = total
        return carry

    lax.fori_loop(0, TRANSFORM // 16, tile, 0)


def spread_taps(taps_in, spread):
    taps = taps_in[...].astype(jnp.float32).astype(jnp.bfloat16)
    index = lax.broadcasted_iota(jnp.int32, (TAPS, 128), 0)
    for p in range(TAPS):
        pick = jnp.where(index == p, 1.0, 0.0).astype(jnp.bfloat16)
        spread[p] = product(taps, pick)


def transform(low, high, table_ref, acc, flat):
    scale = 1.0 / (8192.0 * math.sqrt(TAPS * TRANSFORM))

    def one(s, carry):
        value = acc[s]
        high = value.astype(jnp.bfloat16)
        rest = value - high.astype(jnp.float32)
        mid = rest.astype(jnp.bfloat16)
        low = (rest - mid.astype(jnp.float32)).astype(jnp.bfloat16)
        most = jnp.dot(
            table_ref[: 2 * UNITS, :], jnp.concatenate([high, mid], axis=0),
            preferred_element_type=jnp.float32,
        )
        less = jnp.dot(
            table_ref[2 * UNITS : 3 * UNITS, :], jnp.concatenate([high, low], axis=0),
            preferred_element_type=jnp.float32,
        )
        result = (most[:UNITS] + (less + most[UNITS:])) * scale
        rows = pl.ds(pl.multiple_of(s * UNITS, UNITS), UNITS)
        for half in range(2):
            flat[half, rows, :] = result[:, half * 128 : (half + 1) * 128]
        return carry

    lax.fori_loop(low, high, one, 0)


def gather_correlate(
    raw_ref, taps_in, o_ref, a, b, rim, own_rim, acc, flat, taps_ref, table_ref, rim_sem, y_sem,
    x_sem, s_sem, z_sem, f_sem, out_sem,
):
    r = lax.axis_index("row")
    c = lax.axis_index("col")
    z, yl = r // 2, r % 2
    x, yh, co = c // 4, (c // 2) % 2, c % 2
    flip_r = r + 1 - 2 * yl
    at_x = 2 * x
    place = at_x + yh
    rest = pl.ds(0, SPLIT)
    far = pl.ds(SPLIT, 8 - SPLIT)
    flip_y = c + 2 - 4 * yh
    flip_core = c + 1 - 2 * co
    z_next = [((r + 2) % 16, c), ((r + 14) % 16, c)]
    x_next = [(r, (c + 4 * d) % 16) for d in (1, 2, 3)]
    pair = (flip_r, c)
    cross = (flip_r, flip_y)
    sibling = (r, flip_core)
    across = (r, flip_y)

    barrier = pltpu.get_barrier_semaphore()
    after = (r, (c + 1) % 16)
    before = (r, (c + 15) % 16)
    for peer in z_next + x_next + [pair, cross, sibling, across, after, before]:
        pl.semaphore_signal(barrier, inc=1, device_id=peer, device_id_type=MESH)
    dft_table(table_ref)
    spread_taps(taps_in, taps_ref)
    for s in range(RIM):
        own_rim[s] = raw_ref[(s + 1) * TRANSFORM : (s + 2) * TRANSFORM, :].astype(jnp.bfloat16)
    pl.semaphore_wait(barrier, 11)

    dz = (z - c // 2 + 8) % 8
    main = yl == co
    root = jnp.logical_and(main, dz == 0)
    helper = r == flip_y
    hops = dz + jnp.where(main, 0, 1)
    back = (8 - dz) % 8 + jnp.where(main, 0, 1)
    begin = [LAG * hops // 2, LAG * back // 2]
    more = [dz != 7, dz != 1]
    source = dz == 0
    tail_hops = jnp.minimum(dz, (8 - dz) % 8) + jnp.where(main, 0, 1)
    tail_begin = LAG * tail_hops // 2
    tail_more = [
        jnp.logical_or(source, jnp.logical_and(dz >= 1, dz <= 3)),
        jnp.logical_or(source, dz >= 6),
    ]

    def remote(src, dst, send, recv, peer):
        return pltpu.make_async_remote_copy(
            src_ref=src, dst_ref=dst, send_sem=send, recv_sem=recv, device_id=peer,
            device_id_type=MESH,
        )

    def arrived(dst, sem):
        remote(dst, dst, sem, sem, pair).wait_recv()

    def strip_copy(q):
        frames = pl.ds(STRIPS[q][0], STRIPS[q][1] - STRIPS[q][0])
        return remote(
            own_rim.at[frames], rim.at[frames], out_sem.at[11], rim_sem.at[q], after
        )

    @pl.when(c < 15)
    def _():
        for q in range(len(STRIPS)):
            strip_copy(q).start()

    @pl.when(c == 0)
    def _():
        rim[...] = jnp.zeros_like(rim)

    own_filter(raw_ref, taps_ref, acc)
    done = SPECTRA_DEV
    for q, (low, high) in enumerate(STRIPS):
        @pl.when(c > 0)
        def _():
            strip_copy(q).wait_recv()

        rim_filter(low, high, rim, taps_ref, acc)
        transform(low, done, table_ref, acc, flat)
        done = low

    def send_across(j, carry):
        for e in range(GROUP):
            u = j * GROUP + e
            for half in range(2):
                lanes = pl.ds(half * 128, 128)
                rows = flat[half, pl.ds(u, SPECTRA_DEV, stride=UNITS), :]
                a[u, co, place, :, lanes] = rows.astype(jnp.bfloat16)
        rows = pl.ds(j * GROUP, GROUP)
        remote(
            a.at[rows, co, place], a.at[rows, co, place], out_sem.at[0], y_sem.at[j], across
        ).start()
        return carry

    lax.fori_loop(0, GROUPS, send_across, 0)

    def step(i, carry):
        t = i - 2 * LEAD

        @pl.when(jnp.logical_and(t % GROUP == 0, jnp.logical_and(t >= 0, t < UNITS)))
        def _():
            arrived(a.at[pl.ds(t, GROUP), 1 - co], s_sem.at[t // GROUP])

        for h in range(2):
            u = t - begin[h]

            @pl.when(jnp.logical_and(u >= 0, u < TAIL))
            def _():
                @pl.when(root)
                def _():
                    remote(
                        a.at[u, h], b.at[u, h], out_sem.at[5 + h], z_sem.at[h, u], z_next[h]
                    ).start()
                    remote(
                        a.at[u, h, rest], b.at[u, h, rest], out_sem.at[7 + h], z_sem.at[h, u], pair
                    ).start()
                    pltpu.make_async_copy(a.at[u, h], b.at[u, h], f_sem.at[h, u]).start()

                @pl.when(jnp.logical_and(main, jnp.logical_not(root)))
                def _():
                    arrived(b.at[u, h], z_sem.at[h, u])

                    @pl.when(more[h])
                    def _():
                        remote(
                            b.at[u, h], b.at[u, h], out_sem.at[5 + h], z_sem.at[h, u], z_next[h]
                        ).start()

                    remote(
                        b.at[u, h, far], b.at[u, h, far], out_sem.at[7 + h], f_sem.at[h, u], pair
                    ).start()

                @pl.when(jnp.logical_not(main))
                def _():
                    arrived(b.at[u, h, rest], z_sem.at[h, u])

                    @pl.when(more[h])
                    def _():
                        remote(
                            b.at[u, h, rest], b.at[u, h, rest], out_sem.at[5 + h], z_sem.at[h, u],
                            z_next[h],
                        ).start()

        w = t - tail_begin

        @pl.when(jnp.logical_and(w >= TAIL, w < UNITS))
        def _():
            for h in range(2):
                @pl.when(root)
                def _():
                    for d in range(2):
                        remote(
                            a.at[w, h], b.at[w, h], out_sem.at[12 + d], z_sem.at[h, w], z_next[d]
                        ).start()
                    remote(
                        a.at[w, h, rest], b.at[w, h, rest], out_sem.at[7 + h], z_sem.at[h, w], pair
                    ).start()
                    pltpu.make_async_copy(a.at[w, h], b.at[w, h], f_sem.at[h, w]).start()

                @pl.when(jnp.logical_and(main, jnp.logical_not(root)))
                def _():
                    arrived(b.at[w, h], z_sem.at[h, w])
                    for d in range(2):
                        @pl.when(tail_more[d])
                        def _():
                            remote(
                                b.at[w, h], b.at[w, h], out_sem.at[12 + d], z_sem.at[h, w],
                                z_next[d],
                            ).start()

                    remote(
                        b.at[w, h, far], b.at[w, h, far], out_sem.at[7 + h], f_sem.at[h, w], pair
                    ).start()

                @pl.when(jnp.logical_not(main))
                def _():
                    arrived(b.at[w, h, rest], z_sem.at[h, w])
                    for d in range(2):
                        @pl.when(tail_more[d])
                        def _():
                            remote(
                                b.at[w, h, rest], b.at[w, h, rest], out_sem.at[12 + d],
                                z_sem.at[h, w], z_next[d],
                            ).start()

        @pl.when(jnp.logical_and(helper, jnp.logical_and(t >= 0, t < UNITS)))
        def _():
            for h in range(2):
                remote(
                    a.at[t, h, far], b.at[t, h, far], out_sem.at[9 + h], f_sem.at[h, t], cross
                ).start()

        @pl.when(jnp.logical_and(t % GROUP == 0, t < UNITS))
        def _():
            j = t // GROUP

            m = j + 2 * LEAD // GROUP

            @pl.when(m < GROUPS)
            def _():
                rows = pl.ds(m * GROUP, GROUP)
                arrived(a.at[rows, co, at_x + 1 - yh], y_sem.at[m])
                for d in range(3):
                    remote(
                        a.at[rows, co, pl.ds(at_x, 2)], a.at[rows, co, pl.ds(at_x, 2)], out_sem.at[1 + d],
                        x_sem.at[d, m], x_next[d],
                    ).start()

            n = j + LEAD // GROUP

            @pl.when(jnp.logical_and(n >= 0, n < GROUPS))
            def _():
                rows = pl.ds(n * GROUP, GROUP)
                for d in range(3):
                    arrived(a.at[rows, co, pl.ds((x + 3 - d) % 4 * 2, 2)], x_sem.at[d, n])
                remote(
                    a.at[rows, co], a.at[rows, co], out_sem.at[4], s_sem.at[n], sibling
                ).start()

        first = t - END - 1
        last = t - TAIL_END
        ends = last % 2 == 0
        v = jnp.where(ends, last, first)

        @pl.when(
            jnp.logical_or(
                jnp.logical_and(ends, jnp.logical_and(last >= TAIL, last < UNITS)),
                jnp.logical_and(jnp.logical_not(ends), jnp.logical_and(first >= 0, first < TAIL)),
            )
        )
        def _():
            for e in range(2):
                for h in range(2):
                    @pl.when(root)
                    def _():
                        pltpu.make_async_copy(
                            a.at[v + e, h], b.at[v + e, h], f_sem.at[h, v + e]
                        ).wait()

                    @pl.when(jnp.logical_not(main))
                    def _():
                        arrived(b.at[v + e, h, far], f_sem.at[h, v + e])

            a_re = a[v].reshape(SIDE, SIDE)
            a_im = a[v + 1].reshape(SIDE, SIDE)
            b_re = b[v].reshape(SIDE, SIDE)
            b_im = b[v + 1].reshape(SIDE, SIDE)
            real = product(a_re, b_re) + product(a_im, b_im)
            imag = product(a_im, b_re) - product(a_re, b_im)
            k = v // 2
            o_ref[k, :, 0, :] = (real * (1.0 / SPECTRA)).astype(jnp.bfloat16)
            o_ref[k, :, 1, :] = (imag * (1.0 / SPECTRA)).astype(jnp.bfloat16)

        return carry

    lax.fori_loop(0, max(TAIL + END, UNITS + TAIL_END) + 2 * LEAD, step, 0)

    def left(src, sem):
        remote(src, src, sem, sem, pair).wait_send()

    @pl.when(c < 15)
    def _():
        left(own_rim, out_sem.at[11])

    left(a.at[:, co, place], out_sem.at[0])
    for d in range(3):
        left(a.at[:, co, pl.ds(at_x, 2)], out_sem.at[1 + d])
    left(a.at[:, co], out_sem.at[4])
    for h in range(2):
        @pl.when(jnp.logical_and(main, more[h]))
        def _():
            left(b.at[pl.ds(0, TAIL), h], out_sem.at[5 + h])

        @pl.when(jnp.logical_and(main, tail_more[h]))
        def _():
            left(b.at[pl.ds(TAIL, UNITS - TAIL)], out_sem.at[12 + h])

        @pl.when(jnp.logical_and(jnp.logical_not(main), tail_more[h]))
        def _():
            left(b.at[pl.ds(TAIL, UNITS - TAIL), :, rest], out_sem.at[12 + h])

        @pl.when(jnp.logical_and(jnp.logical_not(main), more[h]))
        def _():
            left(b.at[pl.ds(0, TAIL), h, rest], out_sem.at[5 + h])

        @pl.when(root)
        def _():
            left(b.at[:, h, rest], out_sem.at[7 + h])

        @pl.when(jnp.logical_and(main, jnp.logical_not(root)))
        def _():
            left(b.at[:, h, far], out_sem.at[7 + h])

        @pl.when(helper)
        def _():
            left(a.at[:, h, far], out_sem.at[9 + h])


def body(raw, taps):
    block = (UNITS, 2, 8, SPECTRA_DEV, SIDE)
    dma = pltpu.SemaphoreType.DMA
    return pl.pallas_call(
        gather_correlate,
        out_shape=jax.ShapeDtypeStruct((CHANNELS, SIDE, 2, SIDE), jnp.bfloat16),
        in_specs=[pl.BlockSpec(memory_space=pltpu.VMEM)] * 2,
        out_specs=pl.BlockSpec(memory_space=pltpu.VMEM),
        scratch_shapes=[
            pltpu.VMEM(block, jnp.bfloat16),
            pltpu.VMEM(block, jnp.bfloat16),
            pltpu.VMEM((RIM, TRANSFORM, SIDE), jnp.bfloat16),
            pltpu.VMEM((RIM, TRANSFORM, SIDE), jnp.bfloat16),
            pltpu.VMEM((SPECTRA_DEV, TRANSFORM, SIDE), jnp.float32),
            pltpu.VMEM((2, SPECTRA_DEV * UNITS, 128), jnp.float32),
            pltpu.VMEM((TAPS, TRANSFORM, 128), jnp.float32),
            pltpu.VMEM((3 * UNITS, SIDE), jnp.bfloat16),
            dma((len(STRIPS),)),
            dma((GROUPS,)),
            dma((3, GROUPS)),
            dma((GROUPS,)),
            dma((2, UNITS)),
            dma((2, UNITS)),
            dma((14,)),
        ],
        compiler_params=pltpu.CompilerParams(
            collective_id=0, has_side_effects=True, vmem_limit_bytes=30 * 1024 * 1024
        ),
    )(raw, taps)


def solution(mesh):
    placed = (P("col", "row"), P())
    return jax.shard_map(
        body, mesh=mesh, in_specs=placed, out_specs=P(None, "row", None, "col"), check_vma=False
    )
```

```python
import math

import jax
import jax.numpy as jnp
from jax import lax
from jax.experimental import pallas as pl
from jax.experimental.pallas import tpu as pltpu
from jax.sharding import PartitionSpec as P

CHANNELS = 32
TRANSFORM = 128
TAPS = 16
SPECTRA_DEV = 16
SPECTRA = 256
UNITS = 2 * CHANNELS
SIDE = 256
LAG = 9
SPLIT = 2
GROUP = 2
GROUPS = UNITS // GROUP
LEAD = 6
END = 36
TAIL = UNITS - 6
TAIL_END = 26
RIM = TAPS - 1
STRIPS = [(8, 15), (3, 8), (0, 3)]
MESH = pl.DeviceIdType.MESH


def dft_table(table_ref):
    row = lax.broadcasted_iota(jnp.int32, (UNITS, TRANSFORM), 0)
    sample = lax.broadcasted_iota(jnp.int32, (UNITS, TRANSFORM), 1)
    turn = (sample * ((row >> 1) + 1) + (TRANSFORM // 4) * (row & 1)) & (TRANSFORM - 1)
    turn = jnp.minimum(turn, TRANSFORM - turn)
    rest = jnp.cos(turn.astype(jnp.float32) * (2.0 * math.pi / TRANSFORM))
    parts = []
    for _ in range(3):
        part = rest.astype(jnp.bfloat16)
        rest = rest - part.astype(jnp.float32)
        parts.append(part)
    one, two, three = parts
    for i, pair in enumerate(((one, one), (three, two), (two, one))):
        for half in range(2):
            table_ref[i * UNITS : (i + 1) * UNITS, half * TRANSFORM : (half + 1) * TRANSFORM] = (
                pair[half]
            )


def product(a, b):
    return lax.dot_general(a, b, (((0,), (0,)), ((), ())), preferred_element_type=jnp.float32)


def own_filter(raw_ref, taps_ref, acc):
    def tile(i, carry):
        rows = pl.multiple_of(i * 8, 8)
        for half in range(2):
            lanes = pl.ds(half * 128, 128)
            taps = [taps_ref[p, pl.ds(rows, 8), :] for p in range(TAPS)]
            frames = [
                raw_ref[pl.ds(s * TRANSFORM + rows, 8), lanes].astype(jnp.float32)
                for s in range(SPECTRA_DEV)
            ]
            for s in range(SPECTRA_DEV):
                total = taps[0] * frames[s]
                for p in range(1, s + 1):
                    total = total + taps[p] * frames[s - p]
                acc[s, pl.ds(rows, 8), lanes] = total
        return carry

    lax.fori_loop(0, TRANSFORM // 8, tile, 0)


def rim_filter(low, high, rim, taps_ref, acc):
    def tile(i, carry):
        rows = pl.multiple_of(i * 16, 16)
        for half in range(2):
            lanes = pl.ds(half * 128, 128)
            frames = [
                rim[j, pl.ds(rows, 16), lanes].astype(jnp.float32) for j in range(low, high)
            ]
            for s in range(high):
                total = acc[s, pl.ds(rows, 16), lanes]
                for j in range(max(s, low), high):
                    tap = taps_ref[RIM + s - j, pl.ds(rows, 16), :]
                    total = total + tap * frames[j - low]
                acc[s, pl.ds(rows, 16), lanes] = total
        return carry

    lax.fori_loop(0, TRANSFORM // 16, tile, 0)


def spread_taps(taps_in, spread):
    taps = taps_in[...].astype(jnp.float32).astype(jnp.bfloat16)
    index = lax.broadcasted_iota(jnp.int32, (TAPS, 128), 0)
    for p in range(TAPS):
        pick = jnp.where(index == p, 1.0, 0.0).astype(jnp.bfloat16)
        spread[p] = product(taps, pick)


def transform(low, high, table_ref, acc, flat):
    scale = 1.0 / (8192.0 * math.sqrt(TAPS * TRANSFORM))

    def one(s, carry):
        value = acc[s]
        high = value.astype(jnp.bfloat16)
        rest = value - high.astype(jnp.float32)
        mid = rest.astype(jnp.bfloat16)
        low = (rest - mid.astype(jnp.float32)).astype(jnp.bfloat16)
        most = jnp.dot(
            table_ref[: 2 * UNITS, :], jnp.concatenate([high, mid], axis=0),
            preferred_element_type=jnp.float32,
        )
        less = jnp.dot(
            table_ref[2 * UNITS : 3 * UNITS, :], jnp.concatenate([high, low], axis=0),
            preferred_element_type=jnp.float32,
        )
        result = (most[:UNITS] + (less + most[UNITS:])) * scale
        rows = pl.ds(pl.multiple_of(s * UNITS, UNITS), UNITS)
        for half in range(2):
            flat[half, rows, :] = result[:, half * 128 : (half + 1) * 128]
        return carry

    lax.fori_loop(low, high, one, 0)


def gather_correlate(
    raw_ref, taps_in, o_ref, a, b, rim, own_rim, acc, flat, taps_ref, table_ref, rim_sem, y_sem,
    x_sem, s_sem, z_sem, f_sem, out_sem,
):
    r = lax.axis_index("row")
    c = lax.axis_index("col")
    z, yl = r // 2, r % 2
    x, yh, co = c // 4, (c // 2) % 2, c % 2
    flip_r = r + 1 - 2 * yl
    at_x = 2 * x
    place = at_x + yh
    rest = pl.ds(0, SPLIT)
    far = pl.ds(SPLIT, 8 - SPLIT)
    flip_y = c + 2 - 4 * yh
    flip_core = c + 1 - 2 * co
    z_next = [((r + 2) % 16, c), ((r + 14) % 16, c)]
    x_next = [(r, (c + 4 * d) % 16) for d in (1, 2, 3)]
    pair = (flip_r, c)
    cross = (flip_r, flip_y)
    sibling = (r, flip_core)
    across = (r, flip_y)

    barrier = pltpu.get_barrier_semaphore()
    after = (r, (c + 1) % 16)
    before = (r, (c + 15) % 16)
    for peer in z_next + x_next + [pair, cross, sibling, across, after, before]:
        pl.semaphore_signal(barrier, inc=1, device_id=peer, device_id_type=MESH)
    dft_table(table_ref)
    spread_taps(taps_in, taps_ref)
    for s in range(RIM):
        own_rim[s] = raw_ref[(s + 1) * TRANSFORM : (s + 2) * TRANSFORM, :].astype(jnp.bfloat16)
    pl.semaphore_wait(barrier, 11)

    dz = (z - c // 2 + 8) % 8
    main = yl == co
    root = jnp.logical_and(main, dz == 0)
    helper = r == flip_y
    hops = dz + jnp.where(main, 0, 1)
    back = (8 - dz) % 8 + jnp.where(main, 0, 1)
    begin = [LAG * hops // 2, LAG * back // 2]
    more = [dz != 7, dz != 1]
    source = dz == 0
    tail_hops = jnp.minimum(dz, (8 - dz) % 8) + jnp.where(main, 0, 1)
    tail_begin = LAG * tail_hops // 2
    tail_more = [
        jnp.logical_or(source, jnp.logical_and(dz >= 1, dz <= 3)),
        jnp.logical_or(source, dz >= 6),
    ]

    def remote(src, dst, send, recv, peer):
        return pltpu.make_async_remote_copy(
            src_ref=src, dst_ref=dst, send_sem=send, recv_sem=recv, device_id=peer,
            device_id_type=MESH,
        )

    def arrived(dst, sem):
        remote(dst, dst, sem, sem, pair).wait_recv()

    def strip_copy(q):
        frames = pl.ds(STRIPS[q][0], STRIPS[q][1] - STRIPS[q][0])
        return remote(
            own_rim.at[frames], rim.at[frames], out_sem.at[11], rim_sem.at[q], after
        )

    @pl.when(c < 15)
    def _():
        for q in range(len(STRIPS)):
            strip_copy(q).start()

    @pl.when(c == 0)
    def _():
        rim[...] = jnp.zeros_like(rim)

    own_filter(raw_ref, taps_ref, acc)
    done = SPECTRA_DEV
    for q, (low, high) in enumerate(STRIPS):
        @pl.when(c > 0)
        def _():
            strip_copy(q).wait_recv()

        rim_filter(low, high, rim, taps_ref, acc)
        transform(low, done, table_ref, acc, flat)
        done = low

    def send_across(j, carry):
        for e in range(GROUP):
            u = j * GROUP + e
            for half in range(2):
                lanes = pl.ds(half * 128, 128)
                rows = flat[half, pl.ds(u, SPECTRA_DEV, stride=UNITS), :]
                a[u, co, place, :, lanes] = rows.astype(jnp.bfloat16)
        rows = pl.ds(j * GROUP, GROUP)
        remote(
            a.at[rows, co, place], a.at[rows, co, place], out_sem.at[0], y_sem.at[j], across
        ).start()
        return carry

    lax.fori_loop(0, GROUPS, send_across, 0)

    def step(i, carry):
        t = i - 2 * LEAD

        @pl.when(jnp.logical_and(t % GROUP == 0, jnp.logical_and(t >= 0, t < UNITS)))
        def _():
            arrived(a.at[pl.ds(t, GROUP), 1 - co], s_sem.at[t // GROUP])

        for h in range(2):
            u = t - begin[h]

            @pl.when(jnp.logical_and(u >= 0, u < TAIL))
            def _():
                @pl.when(root)
                def _():
                    remote(
                        a.at[u, h], b.at[u, h], out_sem.at[5 + h], z_sem.at[h, u], z_next[h]
                    ).start()
                    remote(
                        a.at[u, h, rest], b.at[u, h, rest], out_sem.at[7 + h], z_sem.at[h, u], pair
                    ).start()
                    pltpu.make_async_copy(a.at[u, h], b.at[u, h], f_sem.at[h, u]).start()

                @pl.when(jnp.logical_and(main, jnp.logical_not(root)))
                def _():
                    arrived(b.at[u, h], z_sem.at[h, u])

                    @pl.when(more[h])
                    def _():
                        remote(
                            b.at[u, h], b.at[u, h], out_sem.at[5 + h], z_sem.at[h, u], z_next[h]
                        ).start()

                    remote(
                        b.at[u, h, far], b.at[u, h, far], out_sem.at[7 + h], f_sem.at[h, u], pair
                    ).start()

                @pl.when(jnp.logical_not(main))
                def _():
                    arrived(b.at[u, h, rest], z_sem.at[h, u])

                    @pl.when(more[h])
                    def _():
                        remote(
                            b.at[u, h, rest], b.at[u, h, rest], out_sem.at[5 + h], z_sem.at[h, u],
                            z_next[h],
                        ).start()

        w = t - tail_begin

        @pl.when(jnp.logical_and(w >= TAIL, w < UNITS))
        def _():
            for h in range(2):
                @pl.when(root)
                def _():
                    for d in range(2):
                        remote(
                            a.at[w, h], b.at[w, h], out_sem.at[12 + d], z_sem.at[h, w], z_next[d]
                        ).start()
                    remote(
                        a.at[w, h, rest], b.at[w, h, rest], out_sem.at[7 + h], z_sem.at[h, w], pair
                    ).start()
                    pltpu.make_async_copy(a.at[w, h], b.at[w, h], f_sem.at[h, w]).start()

                @pl.when(jnp.logical_and(main, jnp.logical_not(root)))
                def _():
                    arrived(b.at[w, h], z_sem.at[h, w])
                    for d in range(2):
                        @pl.when(tail_more[d])
                        def _():
                            remote(
                                b.at[w, h], b.at[w, h], out_sem.at[12 + d], z_sem.at[h, w],
                                z_next[d],
                            ).start()

                    remote(
                        b.at[w, h, far], b.at[w, h, far], out_sem.at[7 + h], f_sem.at[h, w], pair
                    ).start()

                @pl.when(jnp.logical_not(main))
                def _():
                    arrived(b.at[w, h, rest], z_sem.at[h, w])
                    for d in range(2):
                        @pl.when(tail_more[d])
                        def _():
                            remote(
                                b.at[w, h, rest], b.at[w, h, rest], out_sem.at[12 + d],
                                z_sem.at[h, w], z_next[d],
                            ).start()

        @pl.when(jnp.logical_and(helper, jnp.logical_and(t >= 0, t < UNITS)))
        def _():
            for h in range(2):
                remote(
                    a.at[t, h, far], b.at[t, h, far], out_sem.at[9 + h], f_sem.at[h, t], cross
                ).start()

        @pl.when(jnp.logical_and(t % GROUP == 0, t < UNITS))
        def _():
            j = t // GROUP

            m = j + 2 * LEAD // GROUP

            @pl.when(m < GROUPS)
            def _():
                rows = pl.ds(m * GROUP, GROUP)
                arrived(a.at[rows, co, at_x + 1 - yh], y_sem.at[m])
                for d in range(3):
                    remote(
                        a.at[rows, co, pl.ds(at_x, 2)], a.at[rows, co, pl.ds(at_x, 2)], out_sem.at[1 + d],
                        x_sem.at[d, m], x_next[d],
                    ).start()

            n = j + LEAD // GROUP

            @pl.when(jnp.logical_and(n >= 0, n < GROUPS))
            def _():
                rows = pl.ds(n * GROUP, GROUP)
                for d in range(3):
                    arrived(a.at[rows, co, pl.ds((x + 3 - d) % 4 * 2, 2)], x_sem.at[d, n])
                remote(
                    a.at[rows, co], a.at[rows, co], out_sem.at[4], s_sem.at[n], sibling
                ).start()

        first = t - END - 1
        last = t - TAIL_END
        ends = last % 2 == 0
        v = jnp.where(ends, last, first)

        @pl.when(
            jnp.logical_or(
                jnp.logical_and(ends, jnp.logical_and(last >= TAIL, last < UNITS)),
                jnp.logical_and(jnp.logical_not(ends), jnp.logical_and(first >= 0, first < TAIL)),
            )
        )
        def _():
            for e in range(2):
                for h in range(2):
                    @pl.when(root)
                    def _():
                        pltpu.make_async_copy(
                            a.at[v + e, h], b.at[v + e, h], f_sem.at[h, v + e]
                        ).wait()

                    @pl.when(jnp.logical_not(main))
                    def _():
                        arrived(b.at[v + e, h, far], f_sem.at[h, v + e])

            a_re = a[v].reshape(SIDE, SIDE)
            a_im = a[v + 1].reshape(SIDE, SIDE)
            b_re = b[v].reshape(SIDE, SIDE)
            b_im = b[v + 1].reshape(SIDE, SIDE)
            real = product(a_re, b_re) + product(a_im, b_im)
            imag = product(a_im, b_re) - product(a_re, b_im)
            k = v // 2
            o_ref[k, :, 0, :] = (real * (1.0 / SPECTRA)).astype(jnp.bfloat16)
            o_ref[k, :, 1, :] = (imag * (1.0 / SPECTRA)).astype(jnp.bfloat16)

        return carry

    lax.fori_loop(0, max(TAIL + END, UNITS + TAIL_END) + 2 * LEAD, step, 0)

    def left(src, sem):
        remote(src, src, sem, sem, pair).wait_send()

    @pl.when(c < 15)
    def _():
        left(own_rim, out_sem.at[11])

    left(a.at[:, co, place], out_sem.at[0])
    for d in range(3):
        left(a.at[:, co, pl.ds(at_x, 2)], out_sem.at[1 + d])
    left(a.at[:, co], out_sem.at[4])
    for h in range(2):
        @pl.when(jnp.logical_and(main, more[h]))
        def _():
            left(b.at[pl.ds(0, TAIL), h], out_sem.at[5 + h])

        @pl.when(jnp.logical_and(main, tail_more[h]))
        def _():
            left(b.at[pl.ds(TAIL, UNITS - TAIL)], out_sem.at[12 + h])

        @pl.when(jnp.logical_and(jnp.logical_not(main), tail_more[h]))
        def _():
            left(b.at[pl.ds(TAIL, UNITS - TAIL), :, rest], out_sem.at[12 + h])

        @pl.when(jnp.logical_and(jnp.logical_not(main), more[h]))
        def _():
            left(b.at[pl.ds(0, TAIL), h, rest], out_sem.at[5 + h])

        @pl.when(root)
        def _():
            left(b.at[:, h, rest], out_sem.at[7 + h])

        @pl.when(jnp.logical_and(main, jnp.logical_not(root)))
        def _():
            left(b.at[:, h, far], out_sem.at[7 + h])

        @pl.when(helper)
        def _():
            left(a.at[:, h, far], out_sem.at[9 + h])


def body(raw, taps):
    block = (UNITS, 2, 8, SPECTRA_DEV, SIDE)
    dma = pltpu.SemaphoreType.DMA
    return pl.pallas_call(
        gather_correlate,
        out_shape=jax.ShapeDtypeStruct((CHANNELS, SIDE, 2, SIDE), jnp.bfloat16),
        in_specs=[pl.BlockSpec(memory_space=pltpu.VMEM)] * 2,
        out_specs=pl.BlockSpec(memory_space=pltpu.VMEM),
        scratch_shapes=[
            pltpu.VMEM(block, jnp.bfloat16),
            pltpu.VMEM(block, jnp.bfloat16),
            pltpu.VMEM((RIM, TRANSFORM, SIDE), jnp.bfloat16),
            pltpu.VMEM((RIM, TRANSFORM, SIDE), jnp.bfloat16),
            pltpu.VMEM((SPECTRA_DEV, TRANSFORM, SIDE), jnp.float32),
            pltpu.VMEM((2, SPECTRA_DEV * UNITS, 128), jnp.float32),
            pltpu.VMEM((TAPS, TRANSFORM, 128), jnp.float32),
            pltpu.VMEM((3 * UNITS, SIDE), jnp.bfloat16),
            dma((len(STRIPS),)),
            dma((GROUPS,)),
            dma((3, GROUPS)),
            dma((GROUPS,)),
            dma((2, UNITS)),
            dma((2, UNITS)),
            dma((14,)),
        ],
        compiler_params=pltpu.CompilerParams(
            collective_id=0, has_side_effects=True, vmem_limit_bytes=30 * 1024 * 1024
        ),
    )(raw, taps)


def solution(mesh):
    placed = (P("col", "row"), P())
    return jax.shard_map(
        body, mesh=mesh, in_specs=placed, out_specs=P(None, "row", None, "col"), check_vma=False
    )
```
